128 devices in a mesh: gx: 8 (over z, core), gy: 16 (over y, x).
Axes of the slice: x: 4, y: 4, z: 4, core: 2. Of those that a mesh axis runs over, the one named last changes fastest.
Arguments:
- panels: float32 [3, 1024, 2048], P(None, 'gy', 'gx'), may hold values from -4 to 4
- regrid_tiles: float32 [16, 256, 512], replicated, may hold values from -0.375 to 0.375
- weight_index: int32 [8, 2048, 2], P('gx', 'gy'), may hold values from 0 to 15
- owner: int32 [8, 2048, 1], P('gx', 'gy'), may hold values from 0 to 127; in each aligned block of 128 rows (0 to 127, 128 to 255, ..., all dimensions but the last counted through in order) at most 2 rows name the same one
- surface_type: int32 [2048, 4096], P('gy', 'gx'), may hold values from 0 to 3
- substrate: float32 [8, 2048, 4096], P(None, 'gy', 'gx'), may hold values from 0.5 to 1.5
- conductivity: float32 [8, 2048, 4096], P(None, 'gy', 'gx'), may hold values from 0.5 to 2
- soil_wetness: float32 [8, 16, 256, 512], P('gx', 'gy'), may hold values from 0.1 to 1
- surface_table: float32 [5, 4], replicated, may hold values from 0.3 to 1.5
Outputs:
- skin: float32 [2048, 4096], P('gy', 'gx')
- substrate_out: float32 [8, 2048, 4096], P(None, 'gy', 'gx')
The draws below stay inside these ranges and needn't reach their ends.
Inputs may be any that keep to these rules, and one draw needn't show every extreme that they name: The rows of one device name any one owner at most 2 times; some owner is named exactly 2 times.
All inputs are finite; a program needn't handle non-finite values.
Results may differ from the reference program's by a relative error of at most 0.0003.
Values sent between devices are 32-bit elements; how exact they have to be, the bound alone decides.
A program may use at most 128 MiB of HBM per device.

```python
import math
import jax
import jax.numpy as jnp
import numpy as np
from jax import lax

CX = 512
CY = 128
L = 8
NW = 16
KW = 2
NTYPE = 4
NEWTON = 6
CAP = 2
SLOTS = 256
NX = 4096
NY = 2048
N_GX = 8
N_GY = 16


def with_ends(entries, own_key, least, largest):
    longest = entries.shape.index(max(entries.shape))
    spots = []
    for shift in (0, 1):
        where = [jax.random.randint(jax.random.fold_in(own_key, axis), (), 0, length) for axis, length in enumerate(entries.shape)]
        where[longest] = (where[longest] + shift) % entries.shape[longest]
        spots.append(tuple(where))
    return entries.at[spots[0]].set(least).at[spots[1]].set(largest)


def level_of(own_key, shape, cuts, low, top_value):
    def one(dim, parts):
        heights = jax.random.uniform(jax.random.fold_in(jax.random.fold_in(own_key, 6), dim), (parts,), jnp.float32, low / len(cuts), top_value / len(cuts))
        return jnp.repeat(jnp.exp(heights), shape[dim] // parts).reshape((-1,) + (1,) * (len(shape) - dim - 1))

    loudness = one(*cuts[0])
    for cut in cuts[1:]:
        loudness = loudness * one(*cut)
    return loudness


def assign_block(rng, own, number, rows, count, top, reach, lean):
    ranking = jax.random.permutation(rng, count)
    heavy_load, usual = load_shares(count, rows * top, reach, lean, True), load_shares(count, rows * top, reach, lean, False)
    places = jnp.arange(count)

    def named(sizes, turn):
        used = int((sizes > 0).sum())
        fixed = max(1, used // 4)
        passed = fixed + (places - fixed + turn * (used - fixed)) % max(1, count - fixed)
        return jnp.zeros((count,), jnp.int32).at[ranking[jnp.where(places < fixed, places, passed)]].set(jnp.asarray(sizes, jnp.int32))

    sizes = jnp.where(number % 4 == 0, named(heavy_load, number // 4), named(usual, number - number // 4 - 1))
    mixed = jax.random.permutation(jax.random.fold_in(own, 3), count)
    source_of, taker = mixed[0:count // 2 * 2:2], mixed[1:count // 2 * 2:2]
    room = jnp.minimum(sizes[source_of] - 1, reach - sizes[taker]) // 2
    room = jnp.where((source_of == ranking[0]) | (taker == ranking[0]) | (sizes[taker] == 0), 0, jnp.maximum(room, 0))
    passed = jax.random.randint(jax.random.fold_in(own, 4), (count // 2,), 0, 1 << 20) % (room + 1)
    sizes = sizes.at[source_of].add(-passed).at[taker].add(passed)
    labels = jnp.searchsorted(jnp.cumsum(sizes), jnp.arange(rows * top), side="right").astype(jnp.int32)
    table = labels.reshape(top, rows).T
    table = table[jax.random.permutation(jax.random.fold_in(own, 1), rows)]
    turn = jax.random.randint(jax.random.fold_in(own, 2), (rows, 1), 0, top)
    return jnp.take_along_axis(table, (jnp.arange(top)[None, :] + turn) % top, axis=1)


def load_shares(amount, total, limit, lean, full):
    loads = [(1 << 20) // math.isqrt(grade ** lean) + 1 for grade in range(1, amount + 1)]
    largest = limit if full else min(limit, max(-(-total // amount), total * loads[0] // sum(loads)))
    least = 1 if total - largest >= amount - 1 else 0
    given, spare = [largest] + [least] * (amount - 1), total - largest - least * (amount - 1)
    while spare > 0:
        free = [i for i in range(1, amount) if given[i] < largest] or [i for i in range(1, amount) if given[i] < limit]
        mass, remaining = sum([loads[i] for i in free]), spare
        for i in free:
            more = min(limit - given[i], max(1, remaining * loads[i] // mass), spare)
            given[i] = given[i] + more
            spare = spare - more
    return np.array(given)


def centred(key, dims, scale, bound, pieces=(), held_as=jnp.bfloat16):
    result = scale * jax.random.normal(key, dims, jnp.float32)
    if pieces:
        result = result * level_of(key, dims, pieces, -0.22, 0.18)
    return jnp.clip(result, -bound, bound).astype(held_as)


def setup_inputs(seed: int = 0) -> dict:
    splits = jax.random.split(jax.random.key(seed), 10)
    panels = centred(splits[0], (3, NY // 2, NX // 2), 1.0, 4.0, ((1, 16), (2, 8)), jnp.float32)
    regrid_tiles = centred(splits[1], (NW, CX // 2, CX), (CX // 2) ** -0.5, 0.375, (), jnp.float32)
    weight_index = with_ends(jax.random.randint(splits[2], (N_GX, NY, KW), 0, NW), jax.random.fold_in(splits[2], 1), 0, NW - 1).astype(jnp.int32)
    owner_keys = jax.random.split(jax.random.fold_in(splits[3], 1), N_GX * NY // CY)
    owner_turns = jax.random.permutation(jax.random.fold_in(splits[3], 3), N_GX * NY // CY)
    owner = jax.vmap(lambda own, number: assign_block(jax.random.fold_in(splits[3], 2), own, number, CY, N_GX * N_GY, 1, CAP, 2))(owner_keys, owner_turns).reshape((N_GX, NY, 1))
    surface_type = with_ends(jax.random.randint(splits[4], (NY, NX), 0, NTYPE), jax.random.fold_in(splits[4], 1), 0, NTYPE - 1).astype(jnp.int32)
    substrate = jnp.clip(0.5 + 1.0 * jax.random.uniform(splits[5], (L, NY, NX), jnp.float32) ** level_of(splits[5], (L, NY, NX), ((1, 16), (2, 8)), -0.2, 0.2), 0.5, 1.5)
    conductivity = jnp.clip(jnp.exp(math.log(2.0) - 1.3862944 * jax.random.uniform(splits[6], (L, NY, NX), jnp.float32) ** level_of(splits[6], (L, NY, NX), ((1, 16), (2, 8)), -0.2, 0.2)), 0.5, 2.0)
    soil_wetness = jnp.clip(jnp.exp(math.log(1.0) - 2.3025851 * jax.random.uniform(splits[7], (N_GX, N_GY, SLOTS, CX), jnp.float32) ** level_of(splits[7], (N_GX, N_GY, SLOTS, CX), ((0, 8), (1, 16)), -0.2, 0.2)), 0.1, 1.0)
    surface_table = jnp.clip(jax.random.uniform(splits[8], (5, NTYPE), jnp.float32, 0.3, 1.5), 0.3, 1.5)
    return dict(panels=panels, regrid_tiles=regrid_tiles, weight_index=weight_index, owner=owner, surface_type=surface_type, substrate=substrate, conductivity=conductivity, soil_wetness=soil_wetness, surface_table=surface_table)


def owner_ranks(destination):
    same_owner = destination[:, None] == destination[None, :]
    earlier = jnp.arange(CY)[:, None] > jnp.arange(CY)[None, :]
    return jnp.sum((same_owner & earlier).astype(jnp.int32), axis=1)


def reference(panels, regrid_tiles, weight_index, owner, surface_type, substrate, conductivity, soil_wetness, surface_table):
    devices = N_GX * N_GY
    half_cols = CX // 2
    coarse_rows = jnp.repeat(panels, 2, axis=1)
    tile_panels = coarse_rows.reshape(3, NY, N_GX, half_cols).transpose(2, 1, 0, 3)
    fine_tiles = jnp.zeros((N_GX, NY, 3, CX), jnp.float32)
    for tile_pick in range(NW):
        weight_uses = jnp.sum((weight_index == tile_pick).astype(jnp.float32), axis=2)
        weighted = tile_panels * weight_uses[:, :, None, None]
        fine_tiles = fine_tiles + jnp.einsum("gycp,ps->gycs", weighted, regrid_tiles[tile_pick], precision=lax.Precision.HIGHEST)
    fine_flux = fine_tiles.transpose(2, 1, 0, 3).reshape(3, NY, NX)

    lateral = jnp.roll(substrate, 1, 1) + jnp.roll(substrate, -1, 1) + jnp.roll(substrate, 1, 2) + jnp.roll(substrate, -1, 2) - 4.0 * substrate
    layer_above = jnp.concatenate([substrate[:1], substrate[:-1]], axis=0)
    layer_below = jnp.concatenate([substrate[1:], substrate[-1:]], axis=0)
    vertical = layer_above + layer_below - 2.0 * substrate
    diffused = substrate + 0.08 * conductivity * (lateral + vertical)

    blocks = owner.reshape(devices, CY).astype(jnp.int32)
    tile_rank = lax.map(owner_ranks, blocks).astype(jnp.int32)
    source = jnp.arange(devices, dtype=jnp.int32)[:, None]
    flat_wet = soil_wetness.reshape(devices, devices * CAP, CX)
    wet_tiles = flat_wet[blocks, source * CAP + tile_rank]
    wetness = wet_tiles.reshape(N_GX, N_GY, CY, CX).transpose(1, 2, 0, 3).reshape(NY, NX)

    def lookup(field_row):
        table_sum = jnp.zeros((NY, NX), jnp.float32)
        for surface_kind in range(NTYPE):
            table_sum = table_sum + jnp.where(surface_type == surface_kind, surface_table[field_row, surface_kind], 0.0)
        return table_sum

    absorb, emit, sensible, beta, conduct = [lookup(field_row) for field_row in range(5)]
    air_temp = 1.0 + 0.2 * fine_flux[0]
    vapour = 0.2 * fine_flux[1]
    radiation = 2.0 + 0.3 * fine_flux[2]
    top_layer = diffused[0]
    skin_temp = top_layer
    for iteration in range(NEWTON):
        moisture = beta * wetness * jnp.exp(1.5 * (skin_temp - 1.0))
        magnitude = jnp.abs(skin_temp)
        theta_cube = magnitude * magnitude * magnitude
        residual_f = absorb * radiation - emit * skin_temp * theta_cube - sensible * (skin_temp - air_temp) - (moisture - beta * wetness * vapour) - conduct * (skin_temp - top_layer)
        slope_sum = 4.0 * emit * theta_cube + sensible + 1.5 * moisture + conduct
        skin_temp = skin_temp + 0.4 * residual_f / slope_sum
    ground = conduct * (skin_temp - top_layer)
    substrate_out = diffused.at[0].add(0.5 * ground)
    return skin_temp, substrate_out
```

```python
import jax
import jax.numpy as jnp
from jax import lax
from jax.sharding import PartitionSpec as P

NEWTON = 6


def halo(edge, axis, step):
    count = lax.axis_size(axis)
    return lax.ppermute(edge, axis, [(i, (i + step) % count) for i in range(count)])


def regrid(panels, index_list, tables):
    fields, coarse_rows, half = panels.shape
    tiles, _, width = tables.shape
    flat = panels.reshape(fields * coarse_rows, half)
    total = jnp.zeros((fields, coarse_rows, 2, width), jnp.float32)
    for pick in range(tiles):
        uses = jnp.sum((index_list == pick).astype(jnp.float32), axis=1).reshape(1, coarse_rows, 2, 1)
        product = jnp.dot(flat, tables[pick], precision=lax.Precision.HIGHEST)
        total = total + uses * product.reshape(fields, coarse_rows, 1, width)
    return total.reshape(fields, coarse_rows * 2, width)


def balance(forcing, top_layer, surface_kinds, wetness, surface_table):
    def lookup(field_row):
        table_sum = jnp.zeros(top_layer.shape, jnp.float32)
        for surface_kind in range(surface_table.shape[1]):
            table_sum = table_sum + jnp.where(
                surface_kinds == surface_kind, surface_table[field_row, surface_kind], 0.0
            )
        return table_sum

    absorb, emit, sensible, beta, conduct = [lookup(field_row) for field_row in range(5)]
    air_temp = 1.0 + 0.2 * forcing[0]
    vapour = 0.2 * forcing[1]
    radiation = 2.0 + 0.3 * forcing[2]
    skin_temp = top_layer
    for iteration in range(NEWTON):
        moisture = beta * wetness * jnp.exp(1.5 * (skin_temp - 1.0))
        magnitude = jnp.abs(skin_temp)
        theta_cube = magnitude * magnitude * magnitude
        residual_f = (
            absorb * radiation
            - emit * skin_temp * theta_cube
            - sensible * (skin_temp - air_temp)
            - (moisture - beta * wetness * vapour)
            - conduct * (skin_temp - top_layer)
        )
        slope_sum = 4.0 * emit * theta_cube + sensible + 1.5 * moisture + conduct
        skin_temp = skin_temp + 0.4 * residual_f / slope_sum
    return skin_temp, conduct * (skin_temp - top_layer)


def per_device(
    panels,
    regrid_tiles,
    weight_index,
    owner,
    surface_type,
    substrate,
    conductivity,
    soil_wetness,
    surface_table,
):
    tile_rows = substrate.shape[1]
    handed = lax.all_to_all(soil_wetness[0, 0], ("gx", "gy"), split_axis=0, concat_axis=0, tiled=True)
    north = halo(substrate[:, -1:, :], "gy", 1)
    south = halo(substrate[:, :1, :], "gy", -1)
    west = halo(substrate[:, :, -1:], "gx", 1)
    east = halo(substrate[:, :, :1], "gx", -1)
    lateral = (
        jnp.concatenate([substrate[:, 1:], south], axis=1)
        + jnp.concatenate([north, substrate[:, :-1]], axis=1)
        + jnp.concatenate([substrate[:, :, 1:], east], axis=2)
        + jnp.concatenate([west, substrate[:, :, :-1]], axis=2)
        - 4.0 * substrate
    )
    layer_above = jnp.concatenate([substrate[:1], substrate[:-1]], axis=0)
    layer_below = jnp.concatenate([substrate[1:], substrate[-1:]], axis=0)
    vertical = layer_above + layer_below - 2.0 * substrate
    diffused = substrate + 0.08 * conductivity * (lateral + vertical)
    destination = owner[0, :, 0]
    same_owner = destination[:, None] == destination[None, :]
    earlier = lax.broadcasted_iota(jnp.int32, (tile_rows, tile_rows), 0) > lax.broadcasted_iota(
        jnp.int32, (tile_rows, tile_rows), 1
    )
    tile_rank = jnp.sum((same_owner & earlier).astype(jnp.int32), axis=1)
    wetness = handed[destination * 2 + tile_rank]
    fine_flux = regrid(panels, weight_index[0], regrid_tiles)
    skin, ground = balance(fine_flux, diffused[0], surface_type, wetness, surface_table)
    return skin, diffused.at[0].add(0.5 * ground)


def solution(mesh):
    placed = (
        P(None, "gy", "gx"),
        P(),
        P("gx", "gy", None),
        P("gx", "gy", None),
        P("gy", "gx"),
        P(None, "gy", "gx"),
        P(None, "gy", "gx"),
        P("gx", "gy", None, None),
        P(),
    )
    return jax.shard_map(
        per_device,
        mesh=mesh,
        in_specs=placed,
        out_specs=(P("gy", "gx"), P(None, "gy", "gx")),
        check_vma=False,
    )
```

```python
import jax
import jax.numpy as jnp
from jax import lax
from jax.experimental import pallas as pl
from jax.experimental.pallas import tpu as pltpu
from jax.sharding import PartitionSpec as P

NEWTON = 6
MESH = pl.DeviceIdType.MESH
LANES = 128
EARLY_TILES = 5
STRIP = 16


def split_two(values):
    high = values.astype(jnp.bfloat16)
    low = (values - high.astype(jnp.float32)).astype(jnp.bfloat16)
    return high, low


def make_kernel(n_gx, n_gy, layers, rows, cols, tiles, half):
    devices = n_gx * n_gy
    pairs = rows // 2
    blocks = cols // LANES

    def kernel(
        panels_ref, uses_ref, owner_ref, table_ref,
        soil_hbm, substrate_hbm, conductivity_hbm, kinds_hbm, tiles_hbm,
        skin_hbm, out_hbm,
        soil, send, recv, substrate, conductivity, kinds, weights, coarse, flux,
        diffused, skin, wet,
        send_n, send_s, send_w, send_e, north, south, west, east,
        load_sem, tile_sem, out_sem, a2a_send, a2a_recv, halo_send, halo_recv, own_sem,
    ):
        gx = lax.axis_index("gx")
        gy = lax.axis_index("gy")
        me = gx * n_gy + gy

        loads = [
            pltpu.make_async_copy(soil_hbm, soil, load_sem.at[0]),
            pltpu.make_async_copy(substrate_hbm, substrate, load_sem.at[1]),
            pltpu.make_async_copy(conductivity_hbm, conductivity, load_sem.at[2]),
            pltpu.make_async_copy(kinds_hbm, kinds, load_sem.at[3]),
        ]

        def tile_copy(pick):
            return pltpu.make_async_copy(tiles_hbm.at[pick], weights.at[pick], tile_sem.at[pick])

        loads[0].start()
        loads[1].start()
        for pick in range(tiles):
            tile_copy(pick).start()
        loads[2].start()
        loads[3].start()

        barrier = pltpu.get_barrier_semaphore()

        def greet(offset, carry):
            other = lax.rem(me + offset, devices)
            pl.semaphore_signal(
                barrier, inc=1, device_id=(other // n_gy, lax.rem(other, n_gy)), device_id_type=MESH
            )
            return carry

        lax.fori_loop(1, devices, greet, 0)

        flat = panels_ref[...].reshape(3 * pairs, half)
        high, low = split_two(flat)
        coarse[pl.ds(0, 3 * pairs), :] = high
        coarse[pl.ds(3 * pairs, 3 * pairs), :] = low
        flux[...] = jnp.zeros_like(flux)

        loads[0].wait()
        for block in range(blocks):
            send[pl.ds(block, devices * 2, stride=blocks), :] = soil[:, block * LANES : (block + 1) * LANES]

        loads[1].wait()
        lane = lax.broadcasted_iota(jnp.int32, (rows, LANES), 1)
        gather_w = jnp.zeros((rows, LANES), jnp.float32)
        gather_e = jnp.zeros((rows, LANES), jnp.float32)
        for layer in range(layers):
            send_n[layer : layer + 1, :] = substrate[layer, 0:1, :]
            send_s[layer : layer + 1, :] = substrate[layer, rows - 1 : rows, :]
            left = substrate[layer, :, 0:LANES]
            right = substrate[layer, :, cols - LANES : cols]
            gather_w = jnp.where(lane == layer, left[:, 0:1], gather_w)
            gather_e = jnp.where(lane == layer, right[:, LANES - 1 : LANES], gather_e)
        send_w[...] = gather_w.T[0:layers, :]
        send_e[...] = gather_e.T[0:layers, :]

        def regrid_tile(pick, carry):
            tile_copy(pick).wait()
            uses = [
                sum(
                    jnp.where(uses_ref[pl.ds(parity, pairs, stride=2), :][:, k : k + 1] == pick, 1.0, 0.0)
                    for k in range(2)
                )
                for parity in range(2)
            ]
            for column in range(0, cols, 256):
                w_high, w_low = split_two(weights[pick, :, column : column + 256])
                both = jnp.dot(coarse[...], w_high, preferred_element_type=jnp.float32)
                cross = jnp.dot(
                    coarse[pl.ds(0, 3 * pairs), :], w_low, preferred_element_type=jnp.float32
                )
                product = both[: 3 * pairs] + both[3 * pairs :] + cross
                for field in range(3):
                    part = product[field * pairs : (field + 1) * pairs]
                    for parity in range(2):
                        flux[field, parity, :, column : column + 256] += uses[parity] * part
            return carry

        lax.fori_loop(0, EARLY_TILES, regrid_tile, 0)

        pl.semaphore_wait(barrier, devices - 1)

        def halo_copy(source, target, slot, device_id):
            return pltpu.make_async_remote_copy(
                src_ref=source, dst_ref=target, send_sem=halo_send.at[slot],
                recv_sem=halo_recv.at[slot], device_id=device_id, device_id_type=MESH,
            )

        up = lax.rem(gy + n_gy - 1, n_gy)
        down = lax.rem(gy + 1, n_gy)
        before = lax.rem(gx + n_gx - 1, n_gx)
        after = lax.rem(gx + 1, n_gx)
        halos = [
            halo_copy(send_n, south, 0, (gx, up)),
            halo_copy(send_s, north, 1, (gx, down)),
            halo_copy(send_w, east, 2, (before, gy)),
            halo_copy(send_e, west, 3, (after, gy)),
        ]
        for copy in halos:
            copy.start()

        def hand(offset, carry):
            other = lax.rem(me + offset, devices)
            pltpu.make_async_remote_copy(
                src_ref=send.at[pl.ds(pl.multiple_of(other * 8, 8), 8), :],
                dst_ref=recv.at[pl.ds(pl.multiple_of(me * 8, 8), 8), :],
                send_sem=a2a_send, recv_sem=a2a_recv,
                device_id=(other // n_gy, lax.rem(other, n_gy)), device_id_type=MESH,
            ).start()
            return carry

        lax.fori_loop(1, devices, hand, 0)
        own = pltpu.make_async_copy(
            send.at[pl.ds(pl.multiple_of(me * 8, 8), 8), :],
            recv.at[pl.ds(pl.multiple_of(me * 8, 8), 8), :],
            own_sem,
        )
        own.start()

        lax.fori_loop(EARLY_TILES, tiles, regrid_tile, 0)

        owner_wide = jnp.broadcast_to(owner_ref[...], (rows, rows))
        owner_tall = owner_wide.T
        row_id = lax.broadcasted_iota(jnp.int32, (rows, rows), 0)
        col_id = lax.broadcasted_iota(jnp.int32, (rows, rows), 1)
        twin = jnp.where((owner_wide == owner_tall) & (col_id < row_id), 1.0, 0.0)
        second = jnp.sum(twin, axis=1, keepdims=True) > 0.5
        named = jnp.where(owner_tall == col_id, 1.0, 0.0)
        first_hot = jnp.where(second, 0.0, named).astype(jnp.bfloat16)
        second_hot = jnp.where(second, named, 0.0).astype(jnp.bfloat16)
        hot = jnp.concatenate([first_hot, second_hot], axis=1)

        loads[2].wait()
        loads[3].wait()
        for copy in halos:
            copy.wait()
        west_tall = west[...].T
        east_tall = east[...].T
        strip_row = lax.broadcasted_iota(jnp.int32, (STRIP, cols), 0)
        strip_col = lax.broadcasted_iota(jnp.int32, (STRIP, cols), 1)
        for layer in range(layers):
            for base in range(0, rows, STRIP):
                here = substrate[layer, base : base + STRIP, :]
                if base:
                    row_up = substrate[layer, base - 1 : base, :]
                else:
                    row_up = north[layer : layer + 1, :]
                if base + STRIP < rows:
                    row_down = substrate[layer, base + STRIP : base + STRIP + 1, :]
                else:
                    row_down = south[layer : layer + 1, :]
                lateral = jnp.where(strip_row == 0, row_up, pltpu.roll(here, 1, 0))
                lateral += jnp.where(strip_row == STRIP - 1, row_down, pltpu.roll(here, STRIP - 1, 0))
                lateral += jnp.where(
                    strip_col == 0, west_tall[base : base + STRIP, layer : layer + 1], pltpu.roll(here, 1, 1)
                )
                lateral += jnp.where(
                    strip_col == cols - 1,
                    east_tall[base : base + STRIP, layer : layer + 1],
                    pltpu.roll(here, cols - 1, 1),
                )
                above = substrate[max(layer - 1, 0), base : base + STRIP, :]
                below = substrate[min(layer + 1, layers - 1), base : base + STRIP, :]
                change = (lateral - 4.0 * here) + (above + below - 2.0 * here)
                diffused[layer, base : base + STRIP, :] = (
                    here + 0.08 * conductivity[layer, base : base + STRIP, :] * change
                )
        outs = [
            pltpu.make_async_copy(
                diffused.at[pl.ds(1, layers - 1)], out_hbm.at[pl.ds(1, layers - 1)], out_sem.at[0]
            ),
            pltpu.make_async_copy(diffused.at[0], out_hbm.at[0], out_sem.at[1]),
            pltpu.make_async_copy(skin, skin_hbm, out_sem.at[2]),
        ]
        outs[0].start()

        own.wait()
        everything = pltpu.make_async_remote_copy(
            src_ref=send.at[pl.ds(0, (devices - 1) * 8), :],
            dst_ref=recv.at[pl.ds(0, (devices - 1) * 8), :],
            send_sem=a2a_send, recv_sem=a2a_recv, device_id=(gx, down), device_id_type=MESH,
        )
        everything.wait_recv()
        for block in range(blocks):
            taken = jnp.concatenate(
                [recv[pl.ds(block, devices, stride=8), :], recv[pl.ds(blocks + block, devices, stride=8), :]],
                axis=0,
            )
            t_high, t_low = split_two(taken)
            wet[:, block * LANES : (block + 1) * LANES] = jnp.dot(
                hot, t_high, preferred_element_type=jnp.float32
            ) + jnp.dot(hot, t_low, preferred_element_type=jnp.float32)

        def strip(index, carry):
            base = pl.multiple_of(index * STRIP, STRIP)
            spot = pl.ds(base, STRIP)
            kind = kinds[spot, :]
            is0, is1, is2 = kind == 0, kind == 1, kind == 2

            def lookup(row):
                return jnp.where(
                    is0, table_ref[row, 0],
                    jnp.where(is1, table_ref[row, 1], jnp.where(is2, table_ref[row, 2], table_ref[row, 3])),
                )

            pair = pl.ds(pl.multiple_of(index * (STRIP // 2), STRIP // 2), STRIP // 2)

            def fine(field):
                even = flux[field, 0, pair, :]
                odd = flux[field, 1, pair, :]
                return jnp.stack([even, odd], axis=1).reshape(STRIP, cols)

            absorb, emit, sensible, beta, conduct = [lookup(row) for row in range(5)]
            top = diffused[0, spot, :]
            wetness = beta * wet[spot, :]
            fixed = (
                absorb * (2.0 + 0.3 * fine(2))
                + sensible * (1.0 + 0.2 * fine(0))
                + wetness * (0.2 * fine(1))
                + conduct * top
            )
            linear = sensible + conduct
            temp = top
            for _ in range(NEWTON):
                moisture = wetness * jnp.exp(1.5 * (temp - 1.0))
                size = jnp.abs(temp)
                cube = emit * (size * size * size)
                residual = fixed - temp * (cube + linear) - moisture
                slope = 4.0 * cube + linear + 1.5 * moisture
                temp = temp + 0.4 * residual / slope
            skin[spot, :] = temp
            diffused[0, spot, :] = top + 0.5 * (conduct * (temp - top))
            return carry

        lax.fori_loop(0, rows // STRIP, strip, 0)
        outs[1].start()
        outs[2].start()
        everything.wait_send()
        for copy in outs:
            copy.wait()

    return kernel


def per_device(
    panels,
    regrid_tiles,
    weight_index,
    owner,
    surface_type,
    substrate,
    conductivity,
    soil_wetness,
    surface_table,
):
    n_gx, n_gy = lax.axis_size("gx"), lax.axis_size("gy")
    devices = n_gx * n_gy
    layers, rows, cols = substrate.shape
    tiles, half, _ = regrid_tiles.shape
    f32 = jnp.float32
    vmem = pl.BlockSpec(memory_space=pltpu.VMEM)
    hbm = pl.BlockSpec(memory_space=pl.ANY)
    return pl.pallas_call(
        make_kernel(n_gx, n_gy, layers, rows, cols, tiles, half),
        out_shape=(
            jax.ShapeDtypeStruct((rows, cols), f32),
            jax.ShapeDtypeStruct((layers, rows, cols), f32),
        ),
        in_specs=[vmem, vmem, vmem, pl.BlockSpec(memory_space=pltpu.SMEM)] + [hbm] * 5,
        out_specs=(hbm, hbm),
        scratch_shapes=[
            pltpu.VMEM((2 * devices, cols), f32),
            pltpu.VMEM((8 * devices, LANES), f32),
            pltpu.VMEM((8 * devices, LANES), f32),
            pltpu.VMEM((layers, rows, cols), f32),
            pltpu.VMEM((layers, rows, cols), f32),
            pltpu.VMEM((rows, cols), jnp.int32),
            pltpu.VMEM((tiles, half, cols), f32),
            pltpu.VMEM((3 * rows, half), jnp.bfloat16),
            pltpu.VMEM((3, 2, rows // 2, cols), f32),
            pltpu.VMEM((layers, rows, cols), f32),
            pltpu.VMEM((rows, cols), f32),
            pltpu.VMEM((rows, cols), f32),
            pltpu.VMEM((layers, cols), f32),
            pltpu.VMEM((layers, cols), f32),
            pltpu.VMEM((layers, rows), f32),
            pltpu.VMEM((layers, rows), f32),
            pltpu.VMEM((layers, cols), f32),
            pltpu.VMEM((layers, cols), f32),
            pltpu.VMEM((layers, rows), f32),
            pltpu.VMEM((layers, rows), f32),
            pltpu.SemaphoreType.DMA((4,)),
            pltpu.SemaphoreType.DMA((tiles,)),
            pltpu.SemaphoreType.DMA((3,)),
            pltpu.SemaphoreType.DMA,
            pltpu.SemaphoreType.DMA,
            pltpu.SemaphoreType.DMA((4,)),
            pltpu.SemaphoreType.DMA((4,)),
            pltpu.SemaphoreType.DMA,
        ],
        compiler_params=pltpu.CompilerParams(
            collective_id=0, has_side_effects=True, vmem_limit_bytes=48 * 1024 * 1024
        ),
        name="surface_step",
    )(
        panels, weight_index[0], owner[0].reshape(1, rows), surface_table,
        soil_wetness[0, 0], substrate, conductivity, surface_type, regrid_tiles,
    )


def solution(mesh):
    placed = (
        P(None, "gy", "gx"),
        P(),
        P("gx", "gy", None),
        P("gx", "gy", None),
        P("gy", "gx"),
        P(None, "gy", "gx"),
        P(None, "gy", "gx"),
        P("gx", "gy", None, None),
        P(),
    )
    return jax.shard_map(
        per_device,
        mesh=mesh,
        in_specs=placed,
        out_specs=(P("gy", "gx"), P(None, "gy", "gx")),
        check_vma=False,
    )
```
